256 devices in a mesh: dp: 8 (over z), expert: 32 (over y, x, core).
Axes of the slice: x: 4, y: 4, z: 8, core: 2. Of those that a mesh axis runs over, the one named last changes fastest.
Arguments:
- tokens: bfloat16 [32768, 2048], P(('dp', 'expert')), may hold values from -24 to 24
- expert_ids: int32 [32768, 2], P(('dp', 'expert')), may hold values from 0 to 31, as said below
- slot_index: int32 [32768, 2], P(('dp', 'expert')), may hold values from 0 to 15, as said below
- routing_gates: float32 [32768, 2], P(('dp', 'expert')), may hold values from 0.2 to 1
- grad_out: bfloat16 [32768, 2048], P(('dp', 'expert')), may hold values from -1.5 to 1.5
- w_gate: bfloat16 [32, 2048, 768], P('expert', 'dp'), may hold values from -0.125 to 0.125
- w_up: bfloat16 [32, 2048, 768], P('expert', 'dp'), may hold values from -0.125 to 0.125
- w_down: bfloat16 [32, 2048, 768], P('expert', 'dp'), may hold values from -0.21875 to 0.21875
Outputs:
- layer_out: bfloat16 [32768, 2048], P(('dp', 'expert'))
- grad_tokens: bfloat16 [32768, 2048], P(('dp', 'expert'))
- grad_gates: float32 [32768, 2], P(('dp', 'expert'))
- grad_w_gate: bfloat16 [32, 2048, 768], P('expert', 'dp')
- grad_w_up: bfloat16 [32, 2048, 768], P('expert', 'dp')
- grad_w_down: bfloat16 [32, 2048, 768], P('expert', 'dp')
The draws below stay inside these ranges and needn't reach their ends.
Inputs may be any that keep to these rules, and one draw needn't show every extreme that they name: `expert_ids`: each row names 2 different experts. In each aligned block of 128 rows no expert is named more than 16 times; for each group of 32 blocks in a row, some expert is named exactly 16 times in every block of the group. `slot_index`: within one aligned block of 128 rows, the pairs that name one expert have distinct places, 0 up to their number minus one.
All inputs are finite; a program needn't handle non-finite values.
Results may differ from the reference program's by a relative error of at most 0.014.
Values may be sent and summed in bfloat16 or wider, within the bound.
A program may use at most 128 MiB of HBM per device.

```python
import jax
import jax.numpy as jnp
from jax import lax

D = 2048
FFN = 768
TOPK = 2
TOK_DEV = 128
EXPERTS = 32
CAP = 16
TOKENS = 32768


def routing(key):
    block_count = TOKENS // TOK_DEV
    average = TOK_DEV * TOPK // EXPERTS
    half_count = EXPERTS // 2
    position = jnp.arange(TOK_DEV * TOPK, dtype=jnp.int32)

    def one_block(block_index):
        block_key = jax.random.fold_in(key, block_index)
        key_shift, key_label, key_order = jax.random.split(block_key, 3)
        offsets = jax.random.randint(key_shift, (half_count,), -average, average + 1, dtype=jnp.int32)
        offsets = offsets.at[0].set(average)
        counts = jnp.concatenate([average + offsets, average - offsets])
        run_ends = jnp.cumsum(counts)
        starts = run_ends - counts
        run_index = jnp.sum((position[:, None] >= run_ends[None, :]).astype(jnp.int32), axis=1)
        slot_value = position - starts[run_index]
        group_key = jax.random.fold_in(key, block_count + block_index // EXPERTS)
        full_expert = jax.random.randint(group_key, (), 0, EXPERTS, dtype=jnp.int32)
        labels = jax.random.permutation(key_label, EXPERTS).astype(jnp.int32)
        labels = jnp.where(labels == full_expert, labels[0], labels).at[0].set(full_expert)
        expert_value = labels[run_index]
        token_order = jax.random.permutation(key_order, TOK_DEV).astype(jnp.int32)
        row_index = token_order[position % TOK_DEV]
        column_index = position // TOK_DEV
        expert_table = jnp.zeros((TOK_DEV, TOPK), jnp.int32).at[row_index, column_index].set(expert_value)
        slot_table = jnp.zeros((TOK_DEV, TOPK), jnp.int32).at[row_index, column_index].set(slot_value)
        return (expert_table, slot_table)
    expert_tables, slot_tables = jax.vmap(one_block)(jnp.arange(block_count, dtype=jnp.int32))
    return (expert_tables.reshape(TOKENS, TOPK), slot_tables.reshape(TOKENS, TOPK))


def draw_expert_ids(key, part):
    return routing(jax.random.fold_in(key, 11))[0]


def draw_slot_index(key, part):
    return routing(jax.random.fold_in(key, 11))[1]


def with_spikes(array, own_key, source, target, shards_of, factor):
    owner, partner = [(jnp.arange(array.shape[dim]) // (array.shape[dim] // shards_of)).reshape([-1 if axis == dim else 1 for axis in range(array.ndim)]) for dim in (source, target)]
    chosen = jax.random.permutation(own_key, shards_of)[partner]
    strong = (owner == chosen) | (owner == (partner + shards_of // 2) % shards_of)
    return jnp.where(strong, factor * array, array)


def block_levels(key, shape, shards, low, largest):
    def one(dim, shards_of):
        heights = jax.random.uniform(jax.random.fold_in(jax.random.fold_in(key, 6), dim), (shards_of,), jnp.float32, low / len(shards), largest / len(shards))
        return jnp.repeat(jnp.exp(heights), shape[dim] // shards_of).reshape((-1,) + (1,) * (len(shape) - dim - 1))

    level = one(*shards[0])
    for cut in shards[1:]:
        level = level * one(*cut)
    return level


def gaussian(key, extent, scale, reach, pieces=(), kind=jnp.bfloat16):
    level = block_levels(key, extent, pieces, -0.22, 0.18) if pieces else 1.0
    drawn = jax.random.normal(key, extent, jnp.float32) * scale * level
    return jnp.minimum(jnp.maximum(drawn, -reach), reach).astype(kind)


def gaussian_with(stream_key, shape, spread, limit, cuts, heavy, kind=jnp.bfloat16):
    values = spread * jax.random.normal(stream_key, shape, jnp.float32)
    if cuts:
        values = values * block_levels(stream_key, shape, cuts, -0.22, 0.18)
    return jnp.clip(with_spikes(values, jax.random.fold_in(stream_key, 3), *heavy), -limit, limit).astype(kind)


def setup_inputs(seed: int = 0) -> dict:
    arg_keys = jax.random.split(jax.random.key(seed), 9)
    return {
        "tokens": gaussian_with(arg_keys[0], (TOKENS, D), 1.0, 24.0, ((0, 256),), (0, 1, 256, 6.0)),
        "expert_ids": draw_expert_ids(jax.random.fold_in(arg_keys[8], 71), 0),
        "slot_index": draw_slot_index(jax.random.fold_in(arg_keys[8], 71), 0),
        "routing_gates": jnp.clip(0.2 + 0.8 * jax.random.uniform(arg_keys[3], (TOKENS, TOPK), jnp.float32) ** block_levels(arg_keys[3], (TOKENS, TOPK), ((0, 256),), -0.2, 0.2), 0.2, 1.0),
        "grad_out": gaussian(arg_keys[4], (TOKENS, D), 0.25, 1.5, ((0, 256),)),
        "w_gate": gaussian(arg_keys[5], (EXPERTS, D, FFN), D ** -0.5, 0.125, ((0, 32), (1, 8))),
        "w_up": gaussian(arg_keys[6], (EXPERTS, D, FFN), D ** -0.5, 0.125, ((0, 32), (1, 8))),
        "w_down": gaussian(arg_keys[7], (EXPERTS, D, FFN), FFN ** -0.5, 0.21875, ((0, 32), (1, 8))),
    }


def group_gradient(left_rows, right_rows, group_count):
    left_groups = left_rows.reshape(group_count, -1, left_rows.shape[1]).astype(jnp.float32)
    right_groups = right_rows.reshape(group_count, -1, right_rows.shape[1]).astype(jnp.float32)
    partial_sums = jnp.einsum("grd,grf->gdf", left_groups, right_groups, precision=lax.Precision.HIGHEST)
    rounded = lax.optimization_barrier(partial_sums.astype(jnp.bfloat16))
    return jnp.sum(rounded.astype(jnp.float32), axis=0).astype(jnp.bfloat16)


def reference(tokens, expert_ids, slot_index, routing_gates, grad_out, w_gate, w_up, w_down):
    block_count = TOKENS // TOK_DEV
    group_count = block_count // EXPERTS
    pair_count = TOK_DEV * TOPK
    tok_blocks = tokens.reshape(block_count, TOK_DEV, D)
    grad_blocks = grad_out.reshape(block_count, TOK_DEV, D)
    gate_blocks = routing_gates.reshape(block_count, pair_count)
    target = (expert_ids * CAP + slot_index).reshape(block_count, pair_count).astype(jnp.int32)
    pair_index = jnp.arange(pair_count, dtype=jnp.int32)

    def invert(row_target):
        return jnp.full((EXPERTS * CAP,), -1, jnp.int32).at[row_target].set(pair_index)

    source = jax.vmap(invert)(target)
    block_index = jnp.arange(block_count, dtype=jnp.int32)[:, None]
    flat_block = jnp.broadcast_to(block_index, (block_count, CAP)).reshape(-1)

    def per_expert(totals, expert):
        out_sum, back_sum, gate_grad = totals
        chosen = lax.dynamic_slice_in_dim(source, expert * CAP, CAP, 1)
        occupied = chosen >= 0
        pair_safe = jnp.where(occupied, chosen, 0).astype(jnp.int32)
        token_safe = (pair_safe // TOPK).astype(jnp.int32)
        live_float = jnp.where(occupied, 1.0, 0.0).astype(jnp.float32).reshape(-1)
        zero_row = jnp.zeros((), jnp.bfloat16)
        rows_in = jnp.where(occupied[..., None], tok_blocks[block_index, token_safe], zero_row)
        grad_rows_raw = grad_blocks[block_index, token_safe]
        gate_value = gate_blocks[block_index, pair_safe].reshape(-1) * live_float
        flat_in = rows_in.reshape(-1, D)
        flat_grad_raw = grad_rows_raw.reshape(-1, D)
        flat_grad = (gate_value[:, None] * flat_grad_raw.astype(jnp.float32)).astype(jnp.bfloat16)
        gate_matrix = w_gate[expert]
        up_matrix = w_up[expert]
        down_matrix = w_down[expert]
        gate_pre = jnp.dot(flat_in, gate_matrix, preferred_element_type=jnp.float32)
        up_pre = jnp.dot(flat_in, up_matrix, preferred_element_type=jnp.float32)
        sigmoid_gate = jax.nn.sigmoid(gate_pre)
        active = gate_pre * sigmoid_gate
        hidden = (active * up_pre).astype(jnp.bfloat16)
        expert_out = jnp.dot(hidden, down_matrix.T, preferred_element_type=jnp.float32).astype(jnp.bfloat16)
        down_back = jnp.dot(flat_grad, down_matrix, preferred_element_type=jnp.float32)
        silu_slope = sigmoid_gate * (1.0 + gate_pre * (1.0 - sigmoid_gate))
        grad_gate_pre = (down_back * up_pre * silu_slope).astype(jnp.bfloat16)
        grad_up_pre = (down_back * active).astype(jnp.bfloat16)
        input_back = (jnp.dot(grad_gate_pre, gate_matrix.T, preferred_element_type=jnp.float32)
                      + jnp.dot(grad_up_pre, up_matrix.T, preferred_element_type=jnp.float32)).astype(jnp.bfloat16)
        flat_token = token_safe.reshape(-1)
        flat_pair = pair_safe.reshape(-1)
        out_float = expert_out.astype(jnp.float32)
        out_sum = out_sum.at[flat_block, flat_token].add(gate_value[:, None] * out_float)
        back_sum = back_sum.at[flat_block, flat_token].add(input_back.astype(jnp.float32) * live_float[:, None])
        product = jnp.sum(out_float * flat_grad_raw.astype(jnp.float32), axis=1) * live_float
        gate_grad = gate_grad.at[flat_block, flat_pair].add(product)
        grad_gate_w = group_gradient(flat_in, grad_gate_pre, group_count)
        grad_up_w = group_gradient(flat_in, grad_up_pre, group_count)
        grad_down_w = group_gradient(flat_grad, hidden, group_count)
        return (out_sum, back_sum, gate_grad), (grad_gate_w, grad_up_w, grad_down_w)

    initial = (jnp.zeros((block_count, TOK_DEV, D), jnp.float32),
               jnp.zeros((block_count, TOK_DEV, D), jnp.float32),
               jnp.zeros((block_count, pair_count), jnp.float32))
    totals, grads = lax.scan(per_expert, initial, jnp.arange(EXPERTS, dtype=jnp.int32))
    layer_out = totals[0].reshape(TOKENS, D).astype(jnp.bfloat16)
    grad_tokens = totals[1].reshape(TOKENS, D).astype(jnp.bfloat16)
    grad_gates = totals[2].reshape(TOKENS, TOPK)
    return layer_out, grad_tokens, grad_gates, grads[0], grads[1], grads[2]
```

```python
import functools

import jax
import jax.numpy as jnp
from jax import lax
from jax.experimental import pallas as pl
from jax.experimental.pallas import tpu as pltpu
from jax.sharding import PartitionSpec as P

MESH = pl.DeviceIdType.MESH
F32 = jnp.float32
BF16 = jnp.bfloat16
GATE, UP, DOWN = 0, 1, 2
WIDE = 256


def layer_kernel(
    nz, ne, nx, nc, cap,
    tgt_l, gate_l, tgt_s, gate_s, tok, gout, wg, wu, wd,
    lo, gt, gg, og, ou, od,
    wfull, outx, outg, arrx, arrg, pre, act, prod, back, ret, retb, xt, rsr, rss, onehot, slot_gate,
    own_sem, ag_send, ag_recv, rs_send, rs_recv, a2a_send, a2a_recv,
):
    z = lax.axis_index("dp")
    me = lax.axis_index("expert")
    right, left = lax.rem(z + 1, nz), lax.rem(z + nz - 1, nz)
    peers = (right, left)
    width = tok.shape[1]
    hidden_units = wg.shape[2]
    shard = wg.shape[1]
    half = shard // 2
    rows = outx.shape[0]
    last = nz - 2

    own = pl.ds(pl.multiple_of(z * shard, shard), shard)
    own_copies = [
        pltpu.make_async_copy(ref.at[0], wfull.at[w, own, :], own_sem.at[w])
        for w, ref in ((GATE, wg), (UP, wu), (DOWN, wd))
    ]
    for copy in own_copies:
        copy.start()

    def partner(o, sign):
        oc, ox, oy = lax.rem(o, nc), lax.rem(o // nc, nx), o // (nc * nx)
        c, x, y = lax.rem(me, nc), lax.rem(me // nc, nx), me // (nc * nx)
        ny = ne // (nc * nx)
        c = lax.rem(c + sign * oc + nc, nc)
        x = lax.rem(x + sign * ox + nx, nx)
        y = lax.rem(y + sign * oy + ny, ny)
        return (y * nx + x) * nc + c

    barrier = pltpu.get_barrier_semaphore()
    for peer in peers:
        pl.semaphore_signal(barrier, inc=1, device_id={"dp": peer}, device_id_type=MESH)

    @pl.loop(1, ne)
    def _(o):
        pl.semaphore_signal(barrier, inc=1, device_id={"expert": partner(o, 1)}, device_id_type=MESH)

    slot = lax.broadcasted_iota(jnp.int32, onehot.shape, 0)
    hit0, hit1 = slot == tgt_l[0:1, :], slot == tgt_l[1:2, :]
    onehot[...] = jnp.where(hit0 | hit1, 1.0, 0.0).astype(BF16)
    gates = jnp.where(hit0, gate_l[0:1, :], 0.0) + jnp.where(hit1, gate_l[1:2, :], 0.0)
    slot_gate[...] = jnp.broadcast_to(jnp.sum(gates, axis=1, keepdims=True), slot_gate.shape)

    def columns(n, size=WIDE):
        return pl.ds(pl.multiple_of(n * size, size), size)

    def block(e):
        return pl.ds(pl.multiple_of(e * cap, cap), cap)

    @pl.loop(0, width // WIDE)
    def _(n):
        cols = columns(n)
        outx[:, cols] = jnp.dot(onehot[...], tok[:, cols], preferred_element_type=F32).astype(BF16)

    def piece(w, src, h):
        start = pl.multiple_of(lax.rem(src + 2 * nz, nz) * shard + h * half, half)
        return wfull.at[w, pl.ds(start, half), :]

    def gather_copy(w, h, s, arriving=False):
        hop = s + 1 if arriving else s
        ref = piece(w, z - hop if h == 0 else z + hop, h)
        return pltpu.make_async_remote_copy(
            src_ref=ref, dst_ref=ref,
            send_sem=ag_send.at[w, h, s], recv_sem=ag_recv.at[w, h, s],
            device_id={"dp": peers[h]}, device_id_type=MESH,
        )

    def exchange(src, dst, k, o, arriving=False):
        dest = partner(o, 1)
        landing = partner(o, -1) if arriving else me
        return pltpu.make_async_remote_copy(
            src_ref=src.at[block(dest), :], dst_ref=dst.at[block(landing), :],
            send_sem=a2a_send.at[k, o], recv_sem=a2a_recv.at[k, o],
            device_id={"expert": dest}, device_id_type=MESH,
        )

    def send_rows(src, dst, k):
        @pl.loop(1, ne)
        def _(o):
            exchange(src, dst, k, o).start()

        mine = block(me)
        dst[mine, :] = src[mine, :]

    def await_rows(src, dst, k):
        @pl.loop(1, ne)
        def _(o):
            exchange(src, dst, k, o, arriving=True).wait_recv()

    for copy in own_copies:
        copy.wait()
    pl.semaphore_wait(barrier, ne + 1)
    for w in (GATE, UP, DOWN):
        for h in (0, 1):
            gather_copy(w, h, 0).start()
    send_rows(outx, arrx, 0)

    @pl.loop(0, width // WIDE)
    def _(n):
        cols = columns(n)
        picked = jnp.dot(onehot[...], gout[:, cols], preferred_element_type=F32)
        outg[:, cols] = (picked * slot_gate[:, 0:1]).astype(BF16)

    pre[...] = jnp.zeros_like(pre)
    send_rows(outg, arrg, 1)

    def halves(j):
        a = pl.multiple_of(lax.rem(z - j + 2 * nz, nz) * shard, half)
        b = pl.multiple_of(lax.rem(z + j, nz) * shard + half, half)
        return pl.ds(a, half), pl.ds(b, half)

    def accumulate(w, lhs_ref, j):
        a, b = halves(j)
        lhs = jnp.concatenate([lhs_ref[:, a], lhs_ref[:, b]], axis=1)
        for n in range(hidden_units // WIDE):
            cols = slice(n * WIDE, (n + 1) * WIDE)
            rhs = jnp.concatenate([wfull[w, a, cols], wfull[w, b, cols]], axis=0)
            pre[w, :, cols] += jnp.dot(lhs, rhs, preferred_element_type=F32)

    def accumulate_gate_up(lo_j, hi_j):
        @pl.loop(lo_j, hi_j)
        def _(j):
            @pl.loop(0, 2)
            def _(w):
                accumulate(w, arrx, j)

    def accumulate_down(lo_j, hi_j):
        @pl.loop(lo_j, hi_j)
        def _(j):
            accumulate(DOWN, arrg, j)

    def transpose(k, src):
        @pl.loop(0, width // WIDE)
        def _(n):
            cols = columns(n)
            xt[k, cols, :] = src[:, cols].T

    x_step, g_step = min(3, last - 1), min(5, last - 1)

    @pl.loop(0, last)
    def _(s):
        for w in (GATE, UP, DOWN):
            for h in (0, 1):
                gather_copy(w, h, s, arriving=True).wait_recv()
                gather_copy(w, h, s + 1).start()

        @pl.when(s == x_step)
        def _():
            await_rows(outx, arrx, 0)

        @pl.when(s >= x_step)
        def _():
            accumulate_gate_up(jnp.where(s == x_step, 0, s + 1), s + 2)

        @pl.when(s == x_step)
        def _():
            transpose(0, arrx)

        @pl.when(s == g_step)
        def _():
            await_rows(outg, arrg, 1)
            accumulate_down(0, s + 2)
            transpose(1, arrg)

        @pl.when(s > g_step)
        def _():
            accumulate_down(s + 1, s + 2)

    tile = 64

    def gating(rows_now):
        g = pre[GATE, rows_now, :]
        sig = jax.nn.sigmoid(g)
        return g, pre[UP, rows_now, :], sig, g * sig

    def scatter_copy(w, h, i):
        part = pl.ds(h * half, half)
        return pltpu.make_async_remote_copy(
            src_ref=rss.at[w, i - 1, part, :], dst_ref=rsr.at[w, i - 1, part, :],
            send_sem=rs_send.at[w, h, i - 1], recv_sem=rs_recv.at[w, h, i - 1],
            device_id={"dp": peers[h]}, device_id_type=MESH,
        )

    def scatter_step(w, i, first=False, out=None):
        a, b = halves(i)
        if not first:
            for h in (0, 1):
                scatter_copy(w, h, i - 1).wait_recv()
        k = w // 2
        lhs = jnp.concatenate([xt[k, a, :], xt[k, b, :]], axis=0)
        for n in range(hidden_units // WIDE):
            cols = slice(n * WIDE, (n + 1) * WIDE)
            term = jnp.dot(lhs, act[w, :, cols], preferred_element_type=F32)
            if not first:
                term = term + rsr[w, i - 2, :, cols].astype(F32)
            if out is None:
                rss[w, i - 1, :, cols] = term.astype(BF16)
            else:
                out[0, :, cols] = term.astype(BF16)
        if out is None:
            for h in (0, 1):
                scatter_copy(w, h, i).start()

    for h in (0, 1):
        gather_copy(GATE, h, last, arriving=True).wait_recv()
    for h in (0, 1):
        gather_copy(UP, h, last, arriving=True).wait_recv()
    accumulate_gate_up(nz - 1, nz)

    @pl.loop(0, rows // tile)
    def _(r):
        rows_now = pl.ds(pl.multiple_of(r * tile, tile), tile)
        _, u, _, active = gating(rows_now)
        act[DOWN, rows_now, :] = (active * u).astype(BF16)

    scatter_step(DOWN, 1, first=True)
    for h in (0, 1):
        gather_copy(DOWN, h, last, arriving=True).wait_recv()
    accumulate_down(nz - 1, nz)

    @pl.loop(0, rows // tile)
    def _(r):
        rows_now = pl.ds(pl.multiple_of(r * tile, tile), tile)
        g, u, sig, active = gating(rows_now)
        d = pre[DOWN, rows_now, :]
        slope = sig * (1.0 + g * (1.0 - sig))
        act[GATE, rows_now, :] = (d * u * slope).astype(BF16)
        act[UP, rows_now, :] = (d * active).astype(BF16)

    @pl.loop(0, 2)
    def _(w):
        scatter_step(w, 1, first=True)

    def times_transposed(left, w, n):
        return lax.dot_general(
            left, wfull[w, columns(n), :], (((1,), (1,)), ((), ())), preferred_element_type=F32
        )

    @pl.loop(0, width // WIDE)
    def _(n):
        prod[:, columns(n)] = times_transposed(act[DOWN], DOWN, n).astype(BF16)

    send_rows(prod, ret, 2)

    def input_back():
        @pl.loop(0, width // WIDE)
        def _(n):
            total = times_transposed(act[GATE], GATE, n) + times_transposed(act[UP], UP, n)
            back[:, columns(n)] = total.astype(BF16)

        send_rows(back, retb, 3)

    tok_dev = tok.shape[0]
    slots = lax.broadcasted_iota(jnp.int32, (tok_dev, rows), 1)

    def picks():
        return (
            jnp.where(slots == tgt_s[:, 0:1], 1.0, 0.0).astype(BF16),
            jnp.where(slots == tgt_s[:, 1:2], 1.0, 0.0).astype(BF16),
        )

    def combine_out():
        await_rows(prod, ret, 2)
        pick0, pick1 = picks()
        zero = jnp.zeros((tok_dev, 1), F32)

        def step(n, sums):
            cols = columns(n)
            r0 = jnp.dot(pick0, ret[:, cols], preferred_element_type=F32)
            r1 = jnp.dot(pick1, ret[:, cols], preferred_element_type=F32)
            lo[:, cols] = (gate_s[:, 0:1] * r0 + gate_s[:, 1:2] * r1).astype(BF16)
            cot = gout[:, cols].astype(F32)
            return (
                sums[0] + jnp.sum(r0 * cot, axis=1, keepdims=True),
                sums[1] + jnp.sum(r1 * cot, axis=1, keepdims=True),
            )

        d0, d1 = lax.fori_loop(0, width // WIDE, step, (zero, zero))
        which = lax.broadcasted_iota(jnp.int32, gg.shape, 1)
        gg[...] = jnp.where(which == 0, d0, d1)

    def combine_back():
        await_rows(back, retb, 3)
        pick0, pick1 = picks()

        @pl.loop(0, width // WIDE)
        def _(n):
            cols = columns(n)
            both = pick0 + pick1
            gt[:, cols] = jnp.dot(both, retb[:, cols], preferred_element_type=F32).astype(BF16)

    back_at = 6
    out_at = 3 * (nz - 3) + 3

    @pl.loop(3, 3 * (nz - 1))
    def _(k):
        @pl.when(k == back_at)
        def _():
            input_back()

        @pl.when(k == out_at)
        def _():
            combine_out()

        scatter_step(lax.rem(k + 2, 3), k // 3 + 1)

    combine_back()
    for w, out in ((DOWN, od), (GATE, og), (UP, ou)):
        scatter_step(w, nz, out=out)

    @pl.loop(0, nz - 1)
    def _(s):
        for w in (GATE, UP, DOWN):
            for h in (0, 1):
                gather_copy(w, h, s).wait_send()
                scatter_copy(w, h, s + 1).wait_send()

    @pl.loop(1, ne)
    def _(o):
        for k, (src, dst) in enumerate(((outx, arrx), (outg, arrg), (prod, ret), (back, retb))):
            exchange(src, dst, k, o).wait_send()


def on_device(tokens, expert_ids, slot_index, routing_gates, grad_out, w_gate, w_up, w_down):
    tok_dev, top_k = expert_ids.shape
    width = tokens.shape[1]
    _, shard, hidden_units = w_gate.shape
    nz, ne = lax.axis_size("dp"), lax.axis_size("expert")
    cap = 2 * tok_dev * top_k // ne
    rows = ne * cap
    nc, nx = (2, 4) if ne % 8 == 0 else (1, ne)
    target = expert_ids * cap + slot_index
    vmem = pl.BlockSpec(memory_space=pltpu.VMEM)
    held = pl.BlockSpec(memory_space=pl.ANY)
    wide = lambda *lead: pltpu.VMEM((*lead, width), BF16)
    grad_w = jax.ShapeDtypeStruct(w_gate.shape, BF16)
    dma = pltpu.SemaphoreType.DMA
    return pl.pallas_call(
        functools.partial(layer_kernel, nz, ne, nx, nc, cap),
        out_shape=(
            jax.ShapeDtypeStruct(tokens.shape, BF16),
            jax.ShapeDtypeStruct(tokens.shape, BF16),
            jax.ShapeDtypeStruct(routing_gates.shape, F32),
            grad_w, grad_w, grad_w,
        ),
        in_specs=[vmem] * 6 + [held] * 3,
        out_specs=[vmem] * 6,
        scratch_shapes=[
            pltpu.VMEM((3, width, hidden_units), BF16),
            wide(rows), wide(rows), wide(rows), wide(rows),
            pltpu.VMEM((3, rows, hidden_units), F32),
            pltpu.VMEM((3, rows, hidden_units), BF16),
            wide(rows), wide(rows), wide(rows), wide(rows),
            pltpu.VMEM((2, width, rows), BF16),
            pltpu.VMEM((3, nz - 1, shard, hidden_units), BF16),
            pltpu.VMEM((3, nz - 1, shard, hidden_units), BF16),
            pltpu.VMEM((rows, tok_dev), BF16),
            pltpu.VMEM((rows, 128), F32),
            dma((3,)),
            dma((3, 2, nz - 1)), dma((3, 2, nz - 1)), dma((3, 2, nz - 1)), dma((3, 2, nz - 1)),
            dma((4, ne)), dma((4, ne)),
        ],
        compiler_params=pltpu.CompilerParams(
            collective_id=0, has_side_effects=True, vmem_limit_bytes=67043328
        ),
    )(
        target.T, routing_gates.T, target, routing_gates, tokens, grad_out, w_gate, w_up, w_down
    )


def solution(mesh):
    row = P(("dp", "expert"), None)
    weight = P("expert", "dp", None)
    return jax.shard_map(
        on_device,
        mesh=mesh,
        in_specs=(row,) * 5 + (weight,) * 3,
        out_specs=(row,) * 3 + (weight,) * 3,
        check_vma=False,
    )
```

```python
import functools

import jax
import jax.numpy as jnp
from jax import lax
from jax.experimental import pallas as pl
from jax.experimental.pallas import tpu as pltpu
from jax.sharding import PartitionSpec as P

MESH = pl.DeviceIdType.MESH
F32 = jnp.float32
BF16 = jnp.bfloat16
GATE, UP, DOWN = 0, 1, 2
WIDE = 256
LIMIT = 59 << 20


def layer_kernel(
    nz, ne, nx, nc, cap,
    ids, places, gate_l, tok_in, gout_in, wg, wu, wd,
    lo, gt, gg, og, ou, od,
    wfull, outx, outg, arrx, arrg, pre, act, prod, back, ret, retb, xt, rsr, rss, onehot, slot_gate, term, tok, gout,
    own_sem, row_sem, ag_send, ag_recv, rs_send, rs_recv, a2a_send, a2a_recv,
):
    z = lax.axis_index("dp")
    me = lax.axis_index("expert")
    right, left = lax.rem(z + 1, nz), lax.rem(z + nz - 1, nz)
    peers = (right, left)
    tok_dev, width = tok.shape
    hidden_units = wg.shape[2]
    shard = wg.shape[1]
    half = shard // 2
    rows = outx.shape[0]
    last = nz - 2

    own = pl.ds(pl.multiple_of(z * shard, shard), shard)
    own_copies = [
        pltpu.make_async_copy(ref.at[0], wfull.at[w, own, :], own_sem.at[w])
        for w, ref in ((GATE, wg), (UP, wu), (DOWN, wd))
    ]
    for copy in own_copies:
        copy.start()
    row_copies = [
        pltpu.make_async_copy(ref, to, row_sem.at[k])
        for k, (ref, to) in enumerate(((tok_in, tok), (gout_in, gout)))
    ]

    def partner(o, sign):
        oc, ox, oy = lax.rem(o, nc), lax.rem(o // nc, nx), o // (nc * nx)
        c, x, y = lax.rem(me, nc), lax.rem(me // nc, nx), me // (nc * nx)
        ny = ne // (nc * nx)
        c = lax.rem(c + sign * oc + nc, nc)
        x = lax.rem(x + sign * ox + nx, nx)
        y = lax.rem(y + sign * oy + ny, ny)
        return (y * nx + x) * nc + c

    barrier = pltpu.get_barrier_semaphore()
    for peer in peers:
        pl.semaphore_signal(barrier, inc=1, device_id={"dp": peer}, device_id_type=MESH)

    @pl.loop(1, ne)
    def _(o):
        pl.semaphore_signal(barrier, inc=1, device_id={"expert": partner(o, 1)}, device_id_type=MESH)

    def columns(n, size=WIDE):
        return pl.ds(pl.multiple_of(n * size, size), size)

    def block(e):
        return pl.ds(pl.multiple_of(e * cap, cap), cap)

    def piece(w, src, h):
        start = pl.multiple_of(lax.rem(src + 2 * nz, nz) * shard + h * half, half)
        return wfull.at[w, pl.ds(start, half), :]

    def gather_copy(w, h, s, arriving=False):
        hop = s + 1 if arriving else s
        ref = piece(w, z - hop if h == 0 else z + hop, h)
        return pltpu.make_async_remote_copy(
            src_ref=ref, dst_ref=ref,
            send_sem=ag_send.at[w, h, s], recv_sem=ag_recv.at[w, h, s],
            device_id={"dp": peers[h]}, device_id_type=MESH,
        )

    def exchange(src, dst, k, o, arriving=False):
        dest = partner(o, 1)
        landing = partner(o, -1) if arriving else me
        return pltpu.make_async_remote_copy(
            src_ref=src.at[block(dest), :], dst_ref=dst.at[block(landing), :],
            send_sem=a2a_send.at[k, o], recv_sem=a2a_recv.at[k, o],
            device_id={"expert": dest}, device_id_type=MESH,
        )

    def send_rows(src, dst, k):
        @pl.loop(1, ne)
        def _(o):
            exchange(src, dst, k, o).start()

        mine = block(me)
        dst[mine, :] = src[mine, :]

    def await_rows(src, dst, k):
        @pl.loop(1, ne)
        def _(o):
            exchange(src, dst, k, o, arriving=True).wait_recv()

    for copy in row_copies:
        copy.start()
    for copy in own_copies:
        copy.wait()
    pl.semaphore_wait(barrier, ne + 1)
    for w in (GATE, UP, DOWN):
        for h in (0, 1):
            gather_copy(w, h, 0).start()

    slot = lax.broadcasted_iota(jnp.int32, onehot.shape, 0)
    tgt_l = ids[...] * cap + places[...]
    hit0, hit1 = slot == tgt_l[0:1, :], slot == tgt_l[1:2, :]
    onehot[...] = jnp.where(hit0 | hit1, 1.0, 0.0).astype(BF16)
    gates = jnp.where(hit0, gate_l[0:1, :], 0.0) + jnp.where(hit1, gate_l[1:2, :], 0.0)
    slot_gate[...] = jnp.broadcast_to(jnp.sum(gates, axis=1, keepdims=True), slot_gate.shape)

    for copy in row_copies:
        copy.wait()

    @pl.loop(0, width // WIDE)
    def _(n):
        cols = columns(n)
        outx[:, cols] = jnp.dot(onehot[...], tok[:, cols], preferred_element_type=F32).astype(BF16)

    @pl.loop(0, width // WIDE)
    def _(n):
        cols = columns(n)
        picked = jnp.dot(onehot[...], gout[:, cols], preferred_element_type=F32)
        outg[:, cols] = (picked * slot_gate[:, 0:1]).astype(BF16)

    pre[...] = jnp.zeros_like(pre)
    send_rows(outx, arrx, 0)
    send_rows(outg, arrg, 1)

    def halves(j):
        a = pl.multiple_of(lax.rem(z - j + 2 * nz, nz) * shard, half)
        b = pl.multiple_of(lax.rem(z + j, nz) * shard + half, half)
        return pl.ds(a, half), pl.ds(b, half)

    def accumulate(w, lhs_ref, j):
        a, b = halves(j)
        lhs = jnp.concatenate([lhs_ref[:, a], lhs_ref[:, b]], axis=1)
        for n in range(hidden_units // WIDE):
            cols = slice(n * WIDE, (n + 1) * WIDE)
            rhs = jnp.concatenate([wfull[w, a, cols], wfull[w, b, cols]], axis=0)
            pre[w, :, cols] += jnp.dot(lhs, rhs, preferred_element_type=F32)

    def accumulate_gate_up(lo_j, hi_j):
        @pl.loop(lo_j, hi_j)
        def _(j):
            @pl.loop(0, 2)
            def _(w):
                accumulate(w, arrx, j)

    def accumulate_down(lo_j, hi_j):
        @pl.loop(lo_j, hi_j)
        def _(j):
            accumulate(DOWN, arrg, j)

    def transpose(k, src):
        @pl.loop(0, width // WIDE)
        def _(n):
            cols = columns(n)
            xt[k, cols, :] = src[:, cols].T

    x_step, g_step = min(3, last - 1), min(5, last - 1)

    @pl.loop(0, last)
    def _(s):
        for w in (GATE, UP, DOWN):
            for h in (0, 1):
                gather_copy(w, h, s, arriving=True).wait_recv()
                gather_copy(w, h, s + 1).start()

        @pl.when(s == x_step)
        def _():
            await_rows(outx, arrx, 0)

        @pl.when(s >= x_step)
        def _():
            accumulate_gate_up(jnp.where(s == x_step, 0, s + 1), s + 2)

        @pl.when(s == x_step)
        def _():
            transpose(0, arrx)

        @pl.when(s == g_step)
        def _():
            await_rows(outg, arrg, 1)
            accumulate_down(0, s + 2)
            transpose(1, arrg)

        @pl.when(s > g_step)
        def _():
            accumulate_down(s + 1, s + 2)

    tile = 64

    def gating(rows_now):
        g = pre[GATE, rows_now, :]
        sig = jax.nn.sigmoid(g)
        return g, pre[UP, rows_now, :], sig, g * sig

    def scatter_copy(w, h, i):
        part = pl.ds(h * half, half)
        return pltpu.make_async_remote_copy(
            src_ref=rss.at[w, i - 1, part, :], dst_ref=rsr.at[w, i - 1, part, :],
            send_sem=rs_send.at[w, h, i - 1], recv_sem=rs_recv.at[w, h, i - 1],
            device_id={"dp": peers[h]}, device_id_type=MESH,
        )

    def scatter_step(w, i, first=False, out=None):
        a, b = halves(i)
        k = w // 2
        lhs = jnp.concatenate([xt[k, a, :], xt[k, b, :]], axis=0)
        spans = [slice(n * WIDE, (n + 1) * WIDE) for n in range(hidden_units // WIDE)]
        for cols in spans:
            own_term = jnp.dot(lhs, act[w, :, cols], preferred_element_type=F32)
            if first:
                rss[w, i - 1, :, cols] = own_term.astype(BF16)
            else:
                term[:, cols] = own_term
        if not first:
            for h in (0, 1):
                scatter_copy(w, h, i - 1).wait_recv()
            for cols in spans:
                total = (term[:, cols] + rsr[w, i - 2, :, cols].astype(F32)).astype(BF16)
                if out is None:
                    rss[w, i - 1, :, cols] = total
                else:
                    out[0, :, cols] = total
        if out is None:
            for h in (0, 1):
                scatter_copy(w, h, i).start()

    for h in (0, 1):
        gather_copy(GATE, h, last, arriving=True).wait_recv()
    accumulate(GATE, arrx, nz - 1)
    for h in (0, 1):
        gather_copy(UP, h, last, arriving=True).wait_recv()
    accumulate(UP, arrx, nz - 1)

    @pl.loop(0, rows // tile)
    def _(r):
        rows_now = pl.ds(pl.multiple_of(r * tile, tile), tile)
        _, u, _, active = gating(rows_now)
        act[DOWN, rows_now, :] = (active * u).astype(BF16)

    scatter_step(DOWN, 1, first=True)
    for h in (0, 1):
        gather_copy(DOWN, h, last, arriving=True).wait_recv()
    accumulate_down(nz - 1, nz)

    @pl.loop(0, rows // tile)
    def _(r):
        rows_now = pl.ds(pl.multiple_of(r * tile, tile), tile)
        g, u, sig, active = gating(rows_now)
        d = pre[DOWN, rows_now, :]
        slope = sig * (1.0 + g * (1.0 - sig))
        act[GATE, rows_now, :] = (d * u * slope).astype(BF16)
        act[UP, rows_now, :] = (d * active).astype(BF16)

    @pl.loop(0, 2)
    def _(w):
        scatter_step(w, 1, first=True)

    def times_transposed(left, w, n):
        return lax.dot_general(
            left, wfull[w, columns(n), :], (((1,), (1,)), ((), ())), preferred_element_type=F32
        )

    @pl.loop(0, width // WIDE)
    def _(n):
        prod[:, columns(n)] = times_transposed(act[DOWN], DOWN, n).astype(BF16)

    send_rows(prod, ret, 2)

    def input_back():
        @pl.loop(0, width // WIDE)
        def _(n):
            total = times_transposed(act[GATE], GATE, n) + times_transposed(act[UP], UP, n)
            back[:, columns(n)] = total.astype(BF16)

        send_rows(back, retb, 3)

    slots = lax.broadcasted_iota(jnp.int32, (tok_dev, rows), 1)

    def column(row):
        return jnp.broadcast_to(row, (tok_dev, tok_dev)).T[:, 0:1]

    def picks():
        tgt = ids[...] * cap + places[...]
        return [
            jnp.where(slots == column(tgt[k : k + 1, :]), 1.0, 0.0).astype(BF16) for k in (0, 1)
        ]

    def combine_out():
        await_rows(prod, ret, 2)
        pick0, pick1 = picks()
        gate0, gate1 = column(gate_l[0:1, :]), column(gate_l[1:2, :])
        zero = jnp.zeros((tok_dev, 1), F32)

        def step(n, sums):
            cols = columns(n)
            r0 = jnp.dot(pick0, ret[:, cols], preferred_element_type=F32)
            r1 = jnp.dot(pick1, ret[:, cols], preferred_element_type=F32)
            lo[:, cols] = (gate0 * r0 + gate1 * r1).astype(BF16)
            cot = gout[:, cols].astype(F32)
            return (
                sums[0] + jnp.sum(r0 * cot, axis=1, keepdims=True),
                sums[1] + jnp.sum(r1 * cot, axis=1, keepdims=True),
            )

        d0, d1 = lax.fori_loop(0, width // WIDE, step, (zero, zero))
        for k, d in enumerate((d0, d1)):
            gg[k : k + 1, :] = jnp.broadcast_to(d, (tok_dev, tok_dev)).T[0:1, :]

    def combine_back():
        await_rows(back, retb, 3)
        pick0, pick1 = picks()

        @pl.loop(0, width // WIDE)
        def _(n):
            cols = columns(n)
            both = pick0 + pick1
            gt[:, cols] = jnp.dot(both, retb[:, cols], preferred_element_type=F32).astype(BF16)

    back_at = 6
    out_at = 3 * (nz - 3) + 3

    @pl.loop(3, 3 * (nz - 1))
    def _(k):
        @pl.when(k == back_at)
        def _():
            input_back()

        @pl.when(k == out_at)
        def _():
            combine_out()

        scatter_step(lax.rem(k + 2, 3), k // 3 + 1)

    combine_back()
    for w, out in ((DOWN, od), (GATE, og), (UP, ou)):
        scatter_step(w, nz, out=out)

    @pl.loop(0, nz - 1)
    def _(s):
        for w in (GATE, UP, DOWN):
            for h in (0, 1):
                gather_copy(w, h, s).wait_send()
                scatter_copy(w, h, s + 1).wait_send()

    @pl.loop(1, ne)
    def _(o):
        for k, (src, dst) in enumerate(((outx, arrx), (outg, arrg), (prod, ret), (back, retb))):
            exchange(src, dst, k, o).wait_send()


def write_kernel(*refs):
    sems = refs[-1]
    count = (len(refs) - 1) // 2
    copies = [
        pltpu.make_async_copy(refs[k], refs[count + k], sems.at[k]) for k in range(count)
    ]
    for copy in copies:
        copy.start()
    for copy in copies:
        copy.wait()


def on_device(tokens, expert_ids, slot_index, routing_gates, grad_out, w_gate, w_up, w_down):
    tok_dev, top_k = expert_ids.shape
    width = tokens.shape[1]
    _, shard, hidden_units = w_gate.shape
    nz, ne = lax.axis_size("dp"), lax.axis_size("expert")
    cap = 2 * tok_dev * top_k // ne
    rows = ne * cap
    nc, nx = (2, 4) if ne % 8 == 0 else (1, ne)
    vmem = pl.BlockSpec(memory_space=pltpu.VMEM)
    held = pl.BlockSpec(memory_space=pl.ANY)
    wide = lambda *lead: pltpu.VMEM((*lead, width), BF16)
    dma = pltpu.SemaphoreType.DMA
    outs = (
        (tokens.shape, BF16),
        (tokens.shape, BF16),
        ((top_k, tok_dev), F32),
        (w_gate.shape, BF16),
        (w_gate.shape, BF16),
        (w_gate.shape, BF16),
    )
    results = pl.pallas_call(
        functools.partial(layer_kernel, nz, ne, nx, nc, cap),
        out_shape=tuple(pltpu.VMEM(*out) for out in outs),
        in_specs=[vmem] * 3 + [held] * 5,
        out_specs=[vmem] * 6,
        scratch_shapes=[
            pltpu.VMEM((3, width, hidden_units), BF16),
            wide(rows), wide(rows), wide(rows), wide(rows),
            pltpu.VMEM((3, rows, hidden_units), F32),
            pltpu.VMEM((3, rows, hidden_units), BF16),
            wide(rows), wide(rows), wide(rows), wide(rows),
            pltpu.VMEM((2, width, rows), BF16),
            pltpu.VMEM((3, nz - 1, shard, hidden_units), BF16),
            pltpu.VMEM((3, nz - 1, shard, hidden_units), BF16),
            pltpu.VMEM((rows, tok_dev), BF16),
            pltpu.VMEM((rows, 128), F32),
            pltpu.VMEM((shard, hidden_units), F32),
            wide(tok_dev), wide(tok_dev),
            dma((3,)), dma((2,)),
            dma((3, 2, nz - 1)), dma((3, 2, nz - 1)), dma((3, 2, nz - 1)), dma((3, 2, nz - 1)),
            dma((4, ne)), dma((4, ne)),
        ],
        compiler_params=pltpu.CompilerParams(
            collective_id=0, has_side_effects=True, vmem_limit_bytes=LIMIT
        ),
    )(expert_ids.T, slot_index.T, routing_gates.T, tokens, grad_out, w_gate, w_up, w_down)
    layer_out, grad_tokens, grad_gates, *grads = pl.pallas_call(
        write_kernel,
        out_shape=tuple(jax.ShapeDtypeStruct(*out) for out in outs),
        in_specs=[vmem] * 6,
        out_specs=[held] * 6,
        scratch_shapes=[dma((6,))],
        compiler_params=pltpu.CompilerParams(vmem_limit_bytes=4 << 20),
    )(*results)
    return layer_out, grad_tokens, grad_gates.T, *grads


def solution(mesh):
    row = P(("dp", "expert"), None)
    weight = P("expert", "dp", None)
    return jax.shard_map(
        on_device,
        mesh=mesh,
        in_specs=(row,) * 5 + (weight,) * 3,
        out_specs=(row,) * 3 + (weight,) * 3,
        check_vma=False,
    )
```

```python
import functools

import jax
import jax.numpy as jnp
from jax import lax
from jax.experimental import pallas as pl
from jax.experimental.pallas import tpu as pltpu
from jax.sharding import PartitionSpec as P

MESH = pl.DeviceIdType.MESH
F32 = jnp.float32
BF16 = jnp.bfloat16
GATE, UP, DOWN = 0, 1, 2
WIDE = 256
LIMIT = 59 << 20


def layer_kernel(
    nz, ne, nx, nc, cap,
    ids, places, gate_l, tok_in, gout_in, wg, wu, wd,
    lo, gt, gg, og, ou, od,
    wfull, outx, outg, arrx, arrg, pre, act, prod, back, ret, retb, xt, rsr, rss, onehot, slot_gate, term, tok, gout,
    near_sem, own_sem, row_sem, ag_send, ag_recv, rs_send, rs_recv, a2a_send, a2a_recv,
):
    z = lax.axis_index("dp")
    me = lax.axis_index("expert")
    right, left = lax.rem(z + 1, nz), lax.rem(z + nz - 1, nz)
    peers = (right, left)
    tok_dev, width = tok.shape
    hidden_units = wg.shape[2]
    shard = wg.shape[1]
    half = shard // 2
    rows = outx.shape[0]
    last = nz - 2

    own = pl.ds(pl.multiple_of(z * shard, shard), shard)
    own_copies = [
        pltpu.make_async_copy(ref.at[0], wfull.at[w, own, :], own_sem.at[w])
        for w, ref in ((GATE, wg), (UP, wu), (DOWN, wd))
    ]
    for copy in own_copies:
        copy.start()
    row_copies = [
        pltpu.make_async_copy(ref, to, row_sem.at[k])
        for k, (ref, to) in enumerate(((tok_in, tok), (gout_in, gout)))
    ]

    def partner(o, sign):
        oc, ox, oy = lax.rem(o, nc), lax.rem(o // nc, nx), o // (nc * nx)
        c, x, y = lax.rem(me, nc), lax.rem(me // nc, nx), me // (nc * nx)
        ny = ne // (nc * nx)
        c = lax.rem(c + sign * oc + nc, nc)
        x = lax.rem(x + sign * ox + nx, nx)
        y = lax.rem(y + sign * oy + ny, ny)
        return (y * nx + x) * nc + c

    barrier = pltpu.get_barrier_semaphore()
    for peer in peers:
        pl.semaphore_signal(barrier, inc=1, device_id={"dp": peer}, device_id_type=MESH)

    ny = ne // (nc * nx)
    near, reach = [], 0
    for size, stride in ((nc, 1), (nx, nc), (ny, nc * nx)):
        here = lax.rem(me // stride, size)
        for step in sorted({1, size - 1} - {0}):
            near.append(me + (lax.rem(here + step, size) - here) * stride)
        reach += size // 2

    def greet(sem):
        for e in near:
            pl.semaphore_signal(sem, inc=1, device_id={"expert": e}, device_id_type=MESH)

    greet(barrier)

    def columns(n, size=WIDE):
        return pl.ds(pl.multiple_of(n * size, size), size)

    def block(e):
        return pl.ds(pl.multiple_of(e * cap, cap), cap)

    def piece(w, src, h):
        start = pl.multiple_of(lax.rem(src + 2 * nz, nz) * shard + h * half, half)
        return wfull.at[w, pl.ds(start, half), :]

    def gather_copy(w, h, s, arriving=False):
        hop = s + 1 if arriving else s
        ref = piece(w, z - hop if h == 0 else z + hop, h)
        return pltpu.make_async_remote_copy(
            src_ref=ref, dst_ref=ref,
            send_sem=ag_send.at[w, h, s], recv_sem=ag_recv.at[w, h, s],
            device_id={"dp": peers[h]}, device_id_type=MESH,
        )

    def exchange(src, dst, k, o, arriving=False):
        dest = partner(o, 1)
        landing = partner(o, -1) if arriving else me
        return pltpu.make_async_remote_copy(
            src_ref=src.at[block(dest), :], dst_ref=dst.at[block(landing), :],
            send_sem=a2a_send.at[k, o], recv_sem=a2a_recv.at[k, o],
            device_id={"expert": dest}, device_id_type=MESH,
        )

    def send_rows(src, dst, k):
        @pl.loop(1, ne)
        def _(o):
            exchange(src, dst, k, o).start()

        mine = block(me)
        dst[mine, :] = src[mine, :]

    def await_rows(src, dst, k):
        @pl.loop(1, ne)
        def _(o):
            exchange(src, dst, k, o, arriving=True).wait_recv()

    for copy in row_copies:
        copy.start()
    for copy in own_copies:
        copy.wait()
    pl.semaphore_wait(barrier, len(near) + 2)
    for w in (GATE, UP, DOWN):
        for h in (0, 1):
            gather_copy(w, h, 0).start()

    for r in range(reach - 1):
        greet(near_sem.at[r])
        pl.semaphore_wait(near_sem.at[r], len(near))

    slot = lax.broadcasted_iota(jnp.int32, onehot.shape, 0)
    tgt_l = ids[...] * cap + places[...]
    hit0, hit1 = slot == tgt_l[0:1, :], slot == tgt_l[1:2, :]
    onehot[...] = jnp.where(hit0 | hit1, 1.0, 0.0).astype(BF16)
    gates = jnp.where(hit0, gate_l[0:1, :], 0.0) + jnp.where(hit1, gate_l[1:2, :], 0.0)
    slot_gate[...] = jnp.broadcast_to(jnp.sum(gates, axis=1, keepdims=True), slot_gate.shape)

    for copy in row_copies:
        copy.wait()

    @pl.loop(0, width // WIDE)
    def _(n):
        cols = columns(n)
        outx[:, cols] = jnp.dot(onehot[...], tok[:, cols], preferred_element_type=F32).astype(BF16)

    @pl.loop(0, width // WIDE)
    def _(n):
        cols = columns(n)
        picked = jnp.dot(onehot[...], gout[:, cols], preferred_element_type=F32)
        outg[:, cols] = (picked * slot_gate[:, 0:1]).astype(BF16)

    pre[...] = jnp.zeros_like(pre)
    send_rows(outx, arrx, 0)
    send_rows(outg, arrg, 1)

    def halves(j):
        a = pl.multiple_of(lax.rem(z - j + 2 * nz, nz) * shard, half)
        b = pl.multiple_of(lax.rem(z + j, nz) * shard + half, half)
        return pl.ds(a, half), pl.ds(b, half)

    def accumulate(w, lhs_ref, j):
        a, b = halves(j)
        lhs = jnp.concatenate([lhs_ref[:, a], lhs_ref[:, b]], axis=1)
        for n in range(hidden_units // WIDE):
            cols = slice(n * WIDE, (n + 1) * WIDE)
            rhs = jnp.concatenate([wfull[w, a, cols], wfull[w, b, cols]], axis=0)
            pre[w, :, cols] += jnp.dot(lhs, rhs, preferred_element_type=F32)

    def accumulate_gate_up(lo_j, hi_j):
        @pl.loop(lo_j, hi_j)
        def _(j):
            @pl.loop(0, 2)
            def _(w):
                accumulate(w, arrx, j)

    def accumulate_down(lo_j, hi_j):
        @pl.loop(lo_j, hi_j)
        def _(j):
            accumulate(DOWN, arrg, j)

    def transpose(k, src):
        @pl.loop(0, width // WIDE)
        def _(n):
            cols = columns(n)
            xt[k, cols, :] = src[:, cols].T

    x_step, g_step = min(3, last - 1), min(5, last - 1)

    @pl.loop(0, last)
    def _(s):
        for w in (GATE, UP, DOWN):
            for h in (0, 1):
                gather_copy(w, h, s, arriving=True).wait_recv()
                gather_copy(w, h, s + 1).start()

        @pl.when(s == x_step)
        def _():
            await_rows(outx, arrx, 0)

        @pl.when(s >= x_step)
        def _():
            accumulate_gate_up(jnp.where(s == x_step, 0, s + 1), s + 2)

        @pl.when(s == x_step)
        def _():
            transpose(0, arrx)

        @pl.when(s == g_step)
        def _():
            await_rows(outg, arrg, 1)
            accumulate_down(0, s + 2)
            transpose(1, arrg)

        @pl.when(s > g_step)
        def _():
            accumulate_down(s + 1, s + 2)

    tile = 64

    def gating(rows_now):
        g = pre[GATE, rows_now, :]
        sig = jax.nn.sigmoid(g)
        return g, pre[UP, rows_now, :], sig, g * sig

    def scatter_copy(w, h, i):
        part = pl.ds(h * half, half)
        return pltpu.make_async_remote_copy(
            src_ref=rss.at[w, i - 1, part, :], dst_ref=rsr.at[w, i - 1, part, :],
            send_sem=rs_send.at[w, h, i - 1], recv_sem=rs_recv.at[w, h, i - 1],
            device_id={"dp": peers[h]}, device_id_type=MESH,
        )

    def scatter_step(w, i, first=False, out=None):
        a, b = halves(i)
        k = w // 2
        lhs = jnp.concatenate([xt[k, a, :], xt[k, b, :]], axis=0)
        spans = [slice(n * WIDE, (n + 1) * WIDE) for n in range(hidden_units // WIDE)]
        for cols in spans:
            own_term = jnp.dot(lhs, act[w, :, cols], preferred_element_type=F32)
            if first:
                rss[w, i - 1, :, cols] = own_term.astype(BF16)
            else:
                term[:, cols] = own_term
        if not first:
            for h in (0, 1):
                scatter_copy(w, h, i - 1).wait_recv()
            for cols in spans:
                total = (term[:, cols] + rsr[w, i - 2, :, cols].astype(F32)).astype(BF16)
                if out is None:
                    rss[w, i - 1, :, cols] = total
                else:
                    out[0, :, cols] = total
        if out is None:
            for h in (0, 1):
                scatter_copy(w, h, i).start()

    for h in (0, 1):
        gather_copy(GATE, h, last, arriving=True).wait_recv()
    accumulate(GATE, arrx, nz - 1)
    for h in (0, 1):
        gather_copy(UP, h, last, arriving=True).wait_recv()
    accumulate(UP, arrx, nz - 1)

    @pl.loop(0, rows // tile)
    def _(r):
        rows_now = pl.ds(pl.multiple_of(r * tile, tile), tile)
        _, u, _, active = gating(rows_now)
        act[DOWN, rows_now, :] = (active * u).astype(BF16)

    scatter_step(DOWN, 1, first=True)
    for h in (0, 1):
        gather_copy(DOWN, h, last, arriving=True).wait_recv()
    accumulate_down(nz - 1, nz)

    @pl.loop(0, rows // tile)
    def _(r):
        rows_now = pl.ds(pl.multiple_of(r * tile, tile), tile)
        g, u, sig, active = gating(rows_now)
        d = pre[DOWN, rows_now, :]
        slope = sig * (1.0 + g * (1.0 - sig))
        act[GATE, rows_now, :] = (d * u * slope).astype(BF16)
        act[UP, rows_now, :] = (d * active).astype(BF16)

    @pl.loop(0, 2)
    def _(w):
        scatter_step(w, 1, first=True)

    def times_transposed(left, w, n):
        return lax.dot_general(
            left, wfull[w, columns(n), :], (((1,), (1,)), ((), ())), preferred_element_type=F32
        )

    @pl.loop(0, width // WIDE)
    def _(n):
        prod[:, columns(n)] = times_transposed(act[DOWN], DOWN, n).astype(BF16)

    send_rows(prod, ret, 2)

    def input_back():
        @pl.loop(0, width // WIDE)
        def _(n):
            total = times_transposed(act[GATE], GATE, n) + times_transposed(act[UP], UP, n)
            back[:, columns(n)] = total.astype(BF16)

        send_rows(back, retb, 3)

    slots = lax.broadcasted_iota(jnp.int32, (tok_dev, rows), 1)

    def column(row):
        return jnp.broadcast_to(row, (tok_dev, tok_dev)).T[:, 0:1]

    def picks():
        tgt = ids[...] * cap + places[...]
        return [
            jnp.where(slots == column(tgt[k : k + 1, :]), 1.0, 0.0).astype(BF16) for k in (0, 1)
        ]

    def combine_out():
        await_rows(prod, ret, 2)
        pick0, pick1 = picks()
        gate0, gate1 = column(gate_l[0:1, :]), column(gate_l[1:2, :])
        zero = jnp.zeros((tok_dev, 1), F32)

        def step(n, sums):
            cols = columns(n)
            r0 = jnp.dot(pick0, ret[:, cols], preferred_element_type=F32)
            r1 = jnp.dot(pick1, ret[:, cols], preferred_element_type=F32)
            lo[:, cols] = (gate0 * r0 + gate1 * r1).astype(BF16)
            cot = gout[:, cols].astype(F32)
            return (
                sums[0] + jnp.sum(r0 * cot, axis=1, keepdims=True),
                sums[1] + jnp.sum(r1 * cot, axis=1, keepdims=True),
            )

        d0, d1 = lax.fori_loop(0, width // WIDE, step, (zero, zero))
        for k, d in enumerate((d0, d1)):
            gg[k : k + 1, :] = jnp.broadcast_to(d, (tok_dev, tok_dev)).T[0:1, :]

    def combine_back():
        await_rows(back, retb, 3)
        pick0, pick1 = picks()

        @pl.loop(0, width // WIDE)
        def _(n):
            cols = columns(n)
            both = pick0 + pick1
            gt[:, cols] = jnp.dot(both, retb[:, cols], preferred_element_type=F32).astype(BF16)

    back_at = 6
    out_at = 3 * (nz - 3) + 3

    @pl.loop(3, 3 * (nz - 1))
    def _(k):
        @pl.when(k == back_at)
        def _():
            input_back()

        @pl.when(k == out_at)
        def _():
            combine_out()

        scatter_step(lax.rem(k + 2, 3), k // 3 + 1)

    combine_back()

    @pl.loop(1, ne)
    def _(o):
        for k, (src, dst) in enumerate(((outx, arrx), (outg, arrg), (prod, ret), (back, retb))):
            exchange(src, dst, k, o).wait_send()

    def sent(s, gathered):
        for w in (GATE, UP, DOWN):
            for h in (0, 1):
                if gathered:
                    gather_copy(w, h, s).wait_send()
                else:
                    scatter_copy(w, h, s + 1).wait_send()

    @pl.loop(0, nz - 1)
    def _(s):
        sent(s, True)

    @pl.loop(0, nz - 2)
    def _(s):
        sent(s, False)

    for w, out in ((DOWN, od), (GATE, og), (UP, ou)):
        scatter_step(w, nz, out=out)
    sent(nz - 2, False)


def write_kernel(*refs):
    sems = refs[-1]
    count = (len(refs) - 1) // 2
    copies = [
        pltpu.make_async_copy(refs[k], refs[count + k], sems.at[k]) for k in range(count)
    ]
    for copy in copies:
        copy.start()
    for copy in copies:
        copy.wait()


def on_device(tokens, expert_ids, slot_index, routing_gates, grad_out, w_gate, w_up, w_down):
    tok_dev, top_k = expert_ids.shape
    width = tokens.shape[1]
    _, shard, hidden_units = w_gate.shape
    nz, ne = lax.axis_size("dp"), lax.axis_size("expert")
    cap = 2 * tok_dev * top_k // ne
    rows = ne * cap
    nc, nx = (2, 4) if ne % 8 == 0 else (1, ne)
    vmem = pl.BlockSpec(memory_space=pltpu.VMEM)
    held = pl.BlockSpec(memory_space=pl.ANY)
    wide = lambda *lead: pltpu.VMEM((*lead, width), BF16)
    dma = pltpu.SemaphoreType.DMA
    outs = (
        (tokens.shape, BF16),
        (tokens.shape, BF16),
        ((top_k, tok_dev), F32),
        (w_gate.shape, BF16),
        (w_gate.shape, BF16),
        (w_gate.shape, BF16),
    )
    results = pl.pallas_call(
        functools.partial(layer_kernel, nz, ne, nx, nc, cap),
        out_shape=tuple(pltpu.VMEM(*out) for out in outs),
        in_specs=[vmem] * 3 + [held] * 5,
        out_specs=[vmem] * 6,
        scratch_shapes=[
            pltpu.VMEM((3, width, hidden_units), BF16),
            wide(rows), wide(rows), wide(rows), wide(rows),
            pltpu.VMEM((3, rows, hidden_units), F32),
            pltpu.VMEM((3, rows, hidden_units), BF16),
            wide(rows), wide(rows), wide(rows), wide(rows),
            pltpu.VMEM((2, width, rows), BF16),
            pltpu.VMEM((3, nz - 1, shard, hidden_units), BF16),
            pltpu.VMEM((3, nz - 1, shard, hidden_units), BF16),
            pltpu.VMEM((rows, tok_dev), BF16),
            pltpu.VMEM((rows, 128), F32),
            pltpu.VMEM((shard, hidden_units), F32),
            wide(tok_dev), wide(tok_dev),
            pltpu.SemaphoreType.REGULAR((8,)),
            dma((3,)), dma((2,)),
            dma((3, 2, nz - 1)), dma((3, 2, nz - 1)), dma((3, 2, nz - 1)), dma((3, 2, nz - 1)),
            dma((4, ne)), dma((4, ne)),
        ],
        compiler_params=pltpu.CompilerParams(
            collective_id=0, has_side_effects=True, vmem_limit_bytes=LIMIT
        ),
    )(expert_ids.T, slot_index.T, routing_gates.T, tokens, grad_out, w_gate, w_up, w_down)
    layer_out, grad_tokens, grad_gates, *grads = pl.pallas_call(
        write_kernel,
        out_shape=tuple(jax.ShapeDtypeStruct(*out) for out in outs),
        in_specs=[vmem] * 6,
        out_specs=[held] * 6,
        scratch_shapes=[dma((6,))],
        compiler_params=pltpu.CompilerParams(vmem_limit_bytes=4 << 20),
    )(*results)
    return layer_out, grad_tokens, grad_gates.T, *grads


def solution(mesh):
    row = P(("dp", "expert"), None)
    weight = P("expert", "dp", None)
    return jax.shard_map(
        on_device,
        mesh=mesh,
        in_specs=(row,) * 5 + (weight,) * 3,
        out_specs=(row,) * 3 + (weight,) * 3,
        check_vma=False,
    )
```

```python
import functools

import jax
import jax.numpy as jnp
from jax import lax
from jax.experimental import pallas as pl
from jax.experimental.pallas import tpu as pltpu
from jax.sharding import PartitionSpec as P

MESH = pl.DeviceIdType.MESH
F32 = jnp.float32
BF16 = jnp.bfloat16
GATE, UP, DOWN = 0, 1, 2
WIDE = 256
LIMIT = 59 << 20


def layer_kernel(
    nz, ne, nx, nc, cap,
    ids_in, places_in, gate_in, tok_in, gout_in, wg, wu, wd,
    lo, gt, gg, og, ou, od,
    wfull, outx, outg, arrx, arrg, pre, act, prod, back, ret, retb, xt, rsr, rss, onehot, slot_gate, term, tok, gout, ids, places, gate_l,
    near_sem, own_sem, row_sem, ag_send, ag_recv, rs_send, rs_recv, a2a_send, a2a_recv,
):
    z = lax.axis_index("dp")
    me = lax.axis_index("expert")
    right, left = lax.rem(z + 1, nz), lax.rem(z + nz - 1, nz)
    peers = (right, left)
    tok_dev, width = tok.shape
    hidden_units = wg.shape[2]
    shard = wg.shape[1]
    half = shard // 2
    rows = outx.shape[0]
    last = nz - 2

    own = pl.ds(pl.multiple_of(z * shard, shard), shard)
    own_copies = [
        pltpu.make_async_copy(ref.at[0], wfull.at[w, own, :], own_sem.at[w])
        for w, ref in ((GATE, wg), (UP, wu), (DOWN, wd))
    ]
    row_copies = [
        pltpu.make_async_copy(ref, to, row_sem.at[k])
        for k, (ref, to) in enumerate(
            (
                (ids_in, ids), (places_in, places), (gate_in, gate_l),
                (tok_in, tok), (gout_in, gout),
            )
        )
    ]

    def partner(o, sign):
        oc, ox, oy = lax.rem(o, nc), lax.rem(o // nc, nx), o // (nc * nx)
        c, x, y = lax.rem(me, nc), lax.rem(me // nc, nx), me // (nc * nx)
        ny = ne // (nc * nx)
        c = lax.rem(c + sign * oc + nc, nc)
        x = lax.rem(x + sign * ox + nx, nx)
        y = lax.rem(y + sign * oy + ny, ny)
        return (y * nx + x) * nc + c

    barrier = pltpu.get_barrier_semaphore()
    for peer in peers:
        pl.semaphore_signal(barrier, inc=1, device_id={"dp": peer}, device_id_type=MESH)

    ny = ne // (nc * nx)
    near, reach = [], 0
    for size, stride in ((nc, 1), (nx, nc), (ny, nc * nx)):
        here = lax.rem(me // stride, size)
        for step in sorted({1, size - 1} - {0}):
            near.append(me + (lax.rem(here + step, size) - here) * stride)
        reach += size // 2

    def greet(sem):
        for e in near:
            pl.semaphore_signal(sem, inc=1, device_id={"expert": e}, device_id_type=MESH)

    greet(barrier)

    def columns(n, size=WIDE):
        return pl.ds(pl.multiple_of(n * size, size), size)

    def block(e):
        return pl.ds(pl.multiple_of(e * cap, cap), cap)

    def piece(w, src, h):
        start = pl.multiple_of(lax.rem(src + 2 * nz, nz) * shard + h * half, half)
        return wfull.at[w, pl.ds(start, half), :]

    def gather_copy(w, h, s, arriving=False, source=None):
        hop = s + 1 if arriving else s
        ref = piece(w, z - hop if h == 0 else z + hop, h)
        return pltpu.make_async_remote_copy(
            src_ref=ref if source is None else source, dst_ref=ref,
            send_sem=ag_send.at[w, h, s], recv_sem=ag_recv.at[w, h, s],
            device_id={"dp": peers[h]}, device_id_type=MESH,
        )

    def exchange(src, dst, k, o, arriving=False):
        dest = partner(o, 1)
        landing = partner(o, -1) if arriving else me
        return pltpu.make_async_remote_copy(
            src_ref=src.at[block(dest), :], dst_ref=dst.at[block(landing), :],
            send_sem=a2a_send.at[k, o], recv_sem=a2a_recv.at[k, o],
            device_id={"expert": dest}, device_id_type=MESH,
        )

    def send_rows(src, dst, k):
        @pl.loop(1, ne)
        def _(o):
            exchange(src, dst, k, o).start()

        mine = block(me)
        dst[mine, :] = src[mine, :]

    def await_rows(src, dst, k):
        @pl.loop(1, ne)
        def _(o):
            exchange(src, dst, k, o, arriving=True).wait_recv()

    pl.semaphore_wait(barrier, len(near) + 2)
    for w, ref in ((GATE, wg), (UP, wu), (DOWN, wd)):
        for h in (0, 1):
            gather_copy(w, h, 0, source=ref.at[0, pl.ds(h * half, half), :]).start()
    for copy in row_copies + own_copies:
        copy.start()

    for r in range(reach - 1):
        greet(near_sem.at[r])
        pl.semaphore_wait(near_sem.at[r], len(near))

    for copy in row_copies + own_copies:
        copy.wait()
    slot = lax.broadcasted_iota(jnp.int32, onehot.shape, 0)
    tgt_l = ids[...] * cap + places[...]
    hit0, hit1 = slot == tgt_l[0:1, :], slot == tgt_l[1:2, :]
    onehot[...] = jnp.where(hit0 | hit1, 1.0, 0.0).astype(BF16)
    gates = jnp.where(hit0, gate_l[0:1, :], 0.0) + jnp.where(hit1, gate_l[1:2, :], 0.0)
    slot_gate[...] = jnp.broadcast_to(jnp.sum(gates, axis=1, keepdims=True), slot_gate.shape)


    @pl.loop(0, width // WIDE)
    def _(n):
        cols = columns(n)
        outx[:, cols] = jnp.dot(onehot[...], tok[:, cols], preferred_element_type=F32).astype(BF16)

    @pl.loop(0, width // WIDE)
    def _(n):
        cols = columns(n)
        picked = jnp.dot(onehot[...], gout[:, cols], preferred_element_type=F32)
        outg[:, cols] = (picked * slot_gate[:, 0:1]).astype(BF16)

    pre[...] = jnp.zeros_like(pre)
    send_rows(outx, arrx, 0)
    send_rows(outg, arrg, 1)

    def halves(j):
        a = pl.multiple_of(lax.rem(z - j + 2 * nz, nz) * shard, half)
        b = pl.multiple_of(lax.rem(z + j, nz) * shard + half, half)
        return pl.ds(a, half), pl.ds(b, half)

    def accumulate(w, lhs_ref, j):
        a, b = halves(j)
        lhs = jnp.concatenate([lhs_ref[:, a], lhs_ref[:, b]], axis=1)
        for n in range(hidden_units // WIDE):
            cols = slice(n * WIDE, (n + 1) * WIDE)
            rhs = jnp.concatenate([wfull[w, a, cols], wfull[w, b, cols]], axis=0)
            pre[w, :, cols] += jnp.dot(lhs, rhs, preferred_element_type=F32)

    def accumulate_gate_up(lo_j, hi_j):
        @pl.loop(lo_j, hi_j)
        def _(j):
            @pl.loop(0, 2)
            def _(w):
                accumulate(w, arrx, j)

    def accumulate_down(lo_j, hi_j):
        @pl.loop(lo_j, hi_j)
        def _(j):
            accumulate(DOWN, arrg, j)

    def transpose(k, src):
        @pl.loop(0, width // WIDE)
        def _(n):
            cols = columns(n)
            xt[k, cols, :] = src[:, cols].T

    x_step, g_step = min(3, last - 1), min(5, last - 1)

    @pl.loop(0, last)
    def _(s):
        for w in (GATE, UP, DOWN):
            for h in (0, 1):
                gather_copy(w, h, s, arriving=True).wait_recv()
                gather_copy(w, h, s + 1).start()

        @pl.when(s == x_step)
        def _():
            await_rows(outx, arrx, 0)

        @pl.when(s >= x_step)
        def _():
            accumulate_gate_up(jnp.where(s == x_step, 0, s + 1), s + 2)

        @pl.when(s == x_step)
        def _():
            transpose(0, arrx)

        @pl.when(s == g_step)
        def _():
            await_rows(outg, arrg, 1)
            accumulate_down(0, s + 2)
            transpose(1, arrg)

        @pl.when(s > g_step)
        def _():
            accumulate_down(s + 1, s + 2)

    tile = 64

    def gating(rows_now):
        g = pre[GATE, rows_now, :]
        sig = jax.nn.sigmoid(g)
        return g, pre[UP, rows_now, :], sig, g * sig

    def scatter_copy(w, h, i):
        part = pl.ds(h * half, half)
        return pltpu.make_async_remote_copy(
            src_ref=rss.at[w, i - 1, part, :], dst_ref=rsr.at[w, i - 1, part, :],
            send_sem=rs_send.at[w, h, i - 1], recv_sem=rs_recv.at[w, h, i - 1],
            device_id={"dp": peers[h]}, device_id_type=MESH,
        )

    def scatter_step(w, i, first=False, out=None):
        a, b = halves(i)
        k = w // 2
        lhs = jnp.concatenate([xt[k, a, :], xt[k, b, :]], axis=0)
        spans = [slice(n * WIDE, (n + 1) * WIDE) for n in range(hidden_units // WIDE)]
        for cols in spans:
            own_term = jnp.dot(lhs, act[w, :, cols], preferred_element_type=F32)
            if first:
                rss[w, i - 1, :, cols] = own_term.astype(BF16)
            else:
                term[:, cols] = own_term
        if not first:
            for h in (0, 1):
                scatter_copy(w, h, i - 1).wait_recv()
            for cols in spans:
                total = (term[:, cols] + rsr[w, i - 2, :, cols].astype(F32)).astype(BF16)
                if out is None:
                    rss[w, i - 1, :, cols] = total
                else:
                    out[0, :, cols] = total
        if out is None:
            for h in (0, 1):
                scatter_copy(w, h, i).start()

    for h in (0, 1):
        gather_copy(GATE, h, last, arriving=True).wait_recv()
    accumulate(GATE, arrx, nz - 1)
    for h in (0, 1):
        gather_copy(UP, h, last, arriving=True).wait_recv()
    accumulate(UP, arrx, nz - 1)

    @pl.loop(0, rows // tile)
    def _(r):
        rows_now = pl.ds(pl.multiple_of(r * tile, tile), tile)
        _, u, _, active = gating(rows_now)
        act[DOWN, rows_now, :] = (active * u).astype(BF16)

    scatter_step(DOWN, 1, first=True)
    for h in (0, 1):
        gather_copy(DOWN, h, last, arriving=True).wait_recv()
    accumulate_down(nz - 1, nz)

    @pl.loop(0, rows // tile)
    def _(r):
        rows_now = pl.ds(pl.multiple_of(r * tile, tile), tile)
        g, u, sig, active = gating(rows_now)
        d = pre[DOWN, rows_now, :]
        slope = sig * (1.0 + g * (1.0 - sig))
        act[GATE, rows_now, :] = (d * u * slope).astype(BF16)
        act[UP, rows_now, :] = (d * active).astype(BF16)

    @pl.loop(0, 2)
    def _(w):
        scatter_step(w, 1, first=True)

    def times_transposed(left, w, n):
        return lax.dot_general(
            left, wfull[w, columns(n), :], (((1,), (1,)), ((), ())), preferred_element_type=F32
        )

    @pl.loop(0, width // WIDE)
    def _(n):
        prod[:, columns(n)] = times_transposed(act[DOWN], DOWN, n).astype(BF16)

    send_rows(prod, ret, 2)

    def input_back():
        @pl.loop(0, width // WIDE)
        def _(n):
            total = times_transposed(act[GATE], GATE, n) + times_transposed(act[UP], UP, n)
            back[:, columns(n)] = total.astype(BF16)

        send_rows(back, retb, 3)

    slots = lax.broadcasted_iota(jnp.int32, (tok_dev, rows), 1)

    def column(row):
        return jnp.broadcast_to(row, (tok_dev, tok_dev)).T[:, 0:1]

    def picks():
        tgt = ids[...] * cap + places[...]
        return [
            jnp.where(slots == column(tgt[k : k + 1, :]), 1.0, 0.0).astype(BF16) for k in (0, 1)
        ]

    def combine_out():
        await_rows(prod, ret, 2)
        pick0, pick1 = picks()
        gate0, gate1 = column(gate_l[0:1, :]), column(gate_l[1:2, :])
        zero = jnp.zeros((tok_dev, 1), F32)

        def step(n, sums):
            cols = columns(n)
            r0 = jnp.dot(pick0, ret[:, cols], preferred_element_type=F32)
            r1 = jnp.dot(pick1, ret[:, cols], preferred_element_type=F32)
            lo[:, cols] = (gate0 * r0 + gate1 * r1).astype(BF16)
            cot = gout[:, cols].astype(F32)
            return (
                sums[0] + jnp.sum(r0 * cot, axis=1, keepdims=True),
                sums[1] + jnp.sum(r1 * cot, axis=1, keepdims=True),
            )

        d0, d1 = lax.fori_loop(0, width // WIDE, step, (zero, zero))
        for k, d in enumerate((d0, d1)):
            gg[k : k + 1, :] = jnp.broadcast_to(d, (tok_dev, tok_dev)).T[0:1, :]

    def combine_back():
        await_rows(back, retb, 3)
        pick0, pick1 = picks()

        @pl.loop(0, width // WIDE)
        def _(n):
            cols = columns(n)
            both = pick0 + pick1
            gt[:, cols] = jnp.dot(both, retb[:, cols], preferred_element_type=F32).astype(BF16)

    back_at = 6
    out_at = 3 * (nz - 3) + 3

    @pl.loop(3, 3 * (nz - 1))
    def _(k):
        @pl.when(k == back_at)
        def _():
            input_back()

        @pl.when(k == out_at)
        def _():
            combine_out()

        scatter_step(lax.rem(k + 2, 3), k // 3 + 1)

    combine_back()

    @pl.loop(1, ne)
    def _(o):
        for k, (src, dst) in enumerate(((outx, arrx), (outg, arrg), (prod, ret), (back, retb))):
            exchange(src, dst, k, o).wait_send()

    def sent(s, gathered):
        for w in (GATE, UP, DOWN):
            for h in (0, 1):
                if gathered:
                    gather_copy(w, h, s).wait_send()
                else:
                    scatter_copy(w, h, s + 1).wait_send()

    @pl.loop(0, nz - 1)
    def _(s):
        sent(s, True)

    @pl.loop(0, nz - 2)
    def _(s):
        sent(s, False)

    for w, out in ((DOWN, od), (GATE, og), (UP, ou)):
        scatter_step(w, nz, out=out)
    sent(nz - 2, False)


def write_kernel(*refs):
    sems = refs[-1]
    count = (len(refs) - 1) // 2
    copies = [
        pltpu.make_async_copy(refs[k], refs[count + k], sems.at[k]) for k in range(count)
    ]
    for copy in copies:
        copy.start()
    for copy in copies:
        copy.wait()


def on_device(tokens, expert_ids, slot_index, routing_gates, grad_out, w_gate, w_up, w_down):
    tok_dev, top_k = expert_ids.shape
    width = tokens.shape[1]
    _, shard, hidden_units = w_gate.shape
    nz, ne = lax.axis_size("dp"), lax.axis_size("expert")
    cap = 2 * tok_dev * top_k // ne
    rows = ne * cap
    nc, nx = (2, 4) if ne % 8 == 0 else (1, ne)
    vmem = pl.BlockSpec(memory_space=pltpu.VMEM)
    held = pl.BlockSpec(memory_space=pl.ANY)
    wide = lambda *lead: pltpu.VMEM((*lead, width), BF16)
    dma = pltpu.SemaphoreType.DMA
    outs = (
        (tokens.shape, BF16),
        (tokens.shape, BF16),
        ((top_k, tok_dev), F32),
        (w_gate.shape, BF16),
        (w_gate.shape, BF16),
        (w_gate.shape, BF16),
    )
    results = pl.pallas_call(
        functools.partial(layer_kernel, nz, ne, nx, nc, cap),
        out_shape=tuple(pltpu.VMEM(*out) for out in outs),
        in_specs=[held] * 8,
        out_specs=[vmem] * 6,
        scratch_shapes=[
            pltpu.VMEM((3, width, hidden_units), BF16),
            wide(rows), wide(rows), wide(rows), wide(rows),
            pltpu.VMEM((3, rows, hidden_units), F32),
            pltpu.VMEM((3, rows, hidden_units), BF16),
            wide(rows), wide(rows), wide(rows), wide(rows),
            pltpu.VMEM((2, width, rows), BF16),
            pltpu.VMEM((3, nz - 1, shard, hidden_units), BF16),
            pltpu.VMEM((3, nz - 1, shard, hidden_units), BF16),
            pltpu.VMEM((rows, tok_dev), BF16),
            pltpu.VMEM((rows, 128), F32),
            pltpu.VMEM((shard, hidden_units), F32),
            wide(tok_dev), wide(tok_dev),
            pltpu.VMEM((top_k, tok_dev), jnp.int32), pltpu.VMEM((top_k, tok_dev), jnp.int32),
            pltpu.VMEM((top_k, tok_dev), F32),
            pltpu.SemaphoreType.REGULAR((8,)),
            dma((3,)), dma((5,)),
            dma((3, 2, nz - 1)), dma((3, 2, nz - 1)), dma((3, 2, nz - 1)), dma((3, 2, nz - 1)),
            dma((4, ne)), dma((4, ne)),
        ],
        compiler_params=pltpu.CompilerParams(
            collective_id=0, has_side_effects=True, vmem_limit_bytes=LIMIT
        ),
    )(expert_ids.T, slot_index.T, routing_gates.T, tokens, grad_out, w_gate, w_up, w_down)
    layer_out, grad_tokens, grad_gates, *grads = pl.pallas_call(
        write_kernel,
        out_shape=tuple(jax.ShapeDtypeStruct(*out) for out in outs),
        in_specs=[vmem] * 6,
        out_specs=[held] * 6,
        scratch_shapes=[dma((6,))],
        compiler_params=pltpu.CompilerParams(vmem_limit_bytes=4 << 20),
    )(*results)
    return layer_out, grad_tokens, grad_gates.T, *grads


def solution(mesh):
    row = P(("dp", "expert"), None)
    weight = P("expert", "dp", None)
    return jax.shard_map(
        on_device,
        mesh=mesh,
        in_specs=(row,) * 5 + (weight,) * 3,
        out_specs=(row,) * 3 + (weight,) * 3,
        check_vma=False,
    )
```

```python
import functools

import jax
import jax.numpy as jnp
from jax import lax
from jax.experimental import pallas as pl
from jax.experimental.pallas import tpu as pltpu
from jax.sharding import PartitionSpec as P

MESH = pl.DeviceIdType.MESH
F32 = jnp.float32
BF16 = jnp.bfloat16
GATE, UP, DOWN = 0, 1, 2
WIDE = 256
LIMIT = 59 << 20


def layer_kernel(
    nz, ne, nx, nc, cap,
    ids_in, places_in, gate_in, tok_in, gout_in, wg, wu, wd,
    lo, gt, gg, og, ou, od,
    wfull, outx, outg, arrx, arrg, pre, act, prod, back, ret, retb, xt, rsr, rss, onehot, slot_gate, term, tok, gout, ids, places, gate_l,
    near_sem, own_sem, row_sem, ag_send, ag_recv, rs_send, rs_recv, a2a_send, a2a_recv,
):
    z = lax.axis_index("dp")
    me = lax.axis_index("expert")
    right, left = lax.rem(z + 1, nz), lax.rem(z + nz - 1, nz)
    peers = (right, left)
    tok_dev, width = tok.shape
    hidden_units = wg.shape[2]
    shard = wg.shape[1]
    half = shard // 2
    rows = outx.shape[0]
    last = nz - 2

    own = pl.ds(pl.multiple_of(z * shard, shard), shard)
    own_copies = [
        pltpu.make_async_copy(ref.at[0], wfull.at[w, own, :], own_sem.at[w])
        for w, ref in ((GATE, wg), (UP, wu), (DOWN, wd))
    ]
    row_copies = [
        pltpu.make_async_copy(ref, to, row_sem.at[k])
        for k, (ref, to) in enumerate(
            (
                (ids_in, ids), (places_in, places), (gate_in, gate_l),
                (tok_in, tok), (gout_in, gout),
            )
        )
    ]

    def partner(o, sign):
        oc, ox, oy = lax.rem(o, nc), lax.rem(o // nc, nx), o // (nc * nx)
        c, x, y = lax.rem(me, nc), lax.rem(me // nc, nx), me // (nc * nx)
        ny = ne // (nc * nx)
        c = lax.rem(c + sign * oc + nc, nc)
        x = lax.rem(x + sign * ox + nx, nx)
        y = lax.rem(y + sign * oy + ny, ny)
        return (y * nx + x) * nc + c

    barrier = pltpu.get_barrier_semaphore()
    for peer in peers:
        pl.semaphore_signal(barrier, inc=1, device_id={"dp": peer}, device_id_type=MESH)

    ny = ne // (nc * nx)
    near, reach = [], 0
    for size, stride in ((nc, 1), (nx, nc), (ny, nc * nx)):
        here = lax.rem(me // stride, size)
        for step in sorted({1, size - 1} - {0}):
            near.append(me + (lax.rem(here + step, size) - here) * stride)
        reach += size // 2

    def greet(sem):
        for e in near:
            pl.semaphore_signal(sem, inc=1, device_id={"expert": e}, device_id_type=MESH)

    greet(barrier)

    def columns(n, size=WIDE):
        return pl.ds(pl.multiple_of(n * size, size), size)

    def block(e):
        return pl.ds(pl.multiple_of(e * cap, cap), cap)

    def piece(w, src, h):
        start = pl.multiple_of(lax.rem(src + 2 * nz, nz) * shard + h * half, half)
        return wfull.at[w, pl.ds(start, half), :]

    def gather_copy(w, h, s, arriving=False, source=None):
        hop = s + 1 if arriving else s
        ref = piece(w, z - hop if h == 0 else z + hop, h)
        return pltpu.make_async_remote_copy(
            src_ref=ref if source is None else source, dst_ref=ref,
            send_sem=ag_send.at[w, h, s], recv_sem=ag_recv.at[w, h, s],
            device_id={"dp": peers[h]}, device_id_type=MESH,
        )

    def exchange(src, dst, k, o, arriving=False):
        dest = partner(o, 1)
        landing = partner(o, -1) if arriving else me
        return pltpu.make_async_remote_copy(
            src_ref=src.at[block(dest), :], dst_ref=dst.at[block(landing), :],
            send_sem=a2a_send.at[k, o], recv_sem=a2a_recv.at[k, o],
            device_id={"expert": dest}, device_id_type=MESH,
        )

    def send_rows(src, dst, k):
        @pl.loop(1, ne)
        def _(o):
            exchange(src, dst, k, o).start()

        mine = block(me)
        dst[mine, :] = src[mine, :]

    def await_rows(src, dst, k):
        @pl.loop(1, ne)
        def _(o):
            exchange(src, dst, k, o, arriving=True).wait_recv()

    pl.semaphore_wait(barrier, len(near) + 2)
    for w, ref in ((GATE, wg), (UP, wu), (DOWN, wd)):
        for h in (0, 1):
            gather_copy(w, h, 0, source=ref.at[0, pl.ds(h * half, half), :]).start()
    for copy in row_copies + own_copies:
        copy.start()

    for r in range(reach - 1):
        greet(near_sem.at[r])
        pl.semaphore_wait(near_sem.at[r], len(near))

    for copy in row_copies + own_copies:
        copy.wait()
    slot = lax.broadcasted_iota(jnp.int32, onehot.shape, 0)
    tgt_l = ids[...] * cap + places[...]
    hit0, hit1 = slot == tgt_l[0:1, :], slot == tgt_l[1:2, :]
    onehot[...] = jnp.where(hit0 | hit1, 1.0, 0.0).astype(BF16)
    gates = jnp.where(hit0, gate_l[0:1, :], 0.0) + jnp.where(hit1, gate_l[1:2, :], 0.0)
    slot_gate[...] = jnp.broadcast_to(jnp.sum(gates, axis=1, keepdims=True), slot_gate.shape)


    @pl.loop(0, width // WIDE)
    def _(n):
        cols = columns(n)
        outx[:, cols] = jnp.dot(onehot[...], tok[:, cols], preferred_element_type=F32).astype(BF16)

    @pl.loop(0, width // WIDE)
    def _(n):
        cols = columns(n)
        picked = jnp.dot(onehot[...], gout[:, cols], preferred_element_type=F32)
        outg[:, cols] = (picked * slot_gate[:, 0:1]).astype(BF16)

    pre[...] = jnp.zeros_like(pre)
    send_rows(outx, arrx, 0)
    send_rows(outg, arrg, 1)

    def halves(j):
        a = pl.multiple_of(lax.rem(z - j + 2 * nz, nz) * shard, half)
        b = pl.multiple_of(lax.rem(z + j, nz) * shard + half, half)
        return pl.ds(a, half), pl.ds(b, half)

    def accumulate(w, lhs_ref, j):
        a, b = halves(j)
        lhs = jnp.concatenate([lhs_ref[:, a], lhs_ref[:, b]], axis=1)
        for n in range(hidden_units // WIDE):
            cols = slice(n * WIDE, (n + 1) * WIDE)
            rhs = jnp.concatenate([wfull[w, a, cols], wfull[w, b, cols]], axis=0)
            pre[w, :, cols] += jnp.dot(lhs, rhs, preferred_element_type=F32)

    def accumulate_gate_up(lo_j, hi_j):
        @pl.loop(lo_j, hi_j)
        def _(j):
            @pl.loop(0, 2)
            def _(w):
                accumulate(w, arrx, j)

    def accumulate_down(lo_j, hi_j):
        @pl.loop(lo_j, hi_j)
        def _(j):
            accumulate(DOWN, arrg, j)

    def transpose(k, src):
        @pl.loop(0, width // WIDE)
        def _(n):
            cols = columns(n)
            xt[k, cols, :] = src[:, cols].T

    x_step, g_step = min(4, last - 1), min(5, last - 1)

    @pl.loop(0, last)
    def _(s):
        for w in (GATE, UP, DOWN):
            for h in (0, 1):
                gather_copy(w, h, s, arriving=True).wait_recv()
                gather_copy(w, h, s + 1).start()

        @pl.when(s == x_step)
        def _():
            await_rows(outx, arrx, 0)

        @pl.when(s >= x_step)
        def _():
            accumulate_gate_up(jnp.where(s == x_step, 0, s + 1), s + 2)

        @pl.when(s == x_step)
        def _():
            transpose(0, arrx)

        @pl.when(s == g_step)
        def _():
            await_rows(outg, arrg, 1)
            accumulate_down(0, s + 2)
            transpose(1, arrg)

        @pl.when(s > g_step)
        def _():
            accumulate_down(s + 1, s + 2)

    tile = 64

    def gating(rows_now):
        g = pre[GATE, rows_now, :]
        sig = jax.nn.sigmoid(g)
        return g, pre[UP, rows_now, :], sig, g * sig

    def scatter_copy(w, h, i):
        part = pl.ds(h * half, half)
        return pltpu.make_async_remote_copy(
            src_ref=rss.at[w, i - 1, part, :], dst_ref=rsr.at[w, i - 1, part, :],
            send_sem=rs_send.at[w, h, i - 1], recv_sem=rs_recv.at[w, h, i - 1],
            device_id={"dp": peers[h]}, device_id_type=MESH,
        )

    def scatter_step(w, i, first=False, out=None):
        a, b = halves(i)
        k = w // 2
        lhs = jnp.concatenate([xt[k, a, :], xt[k, b, :]], axis=0)
        spans = [slice(n * WIDE, (n + 1) * WIDE) for n in range(hidden_units // WIDE)]
        for cols in spans:
            own_term = jnp.dot(lhs, act[w, :, cols], preferred_element_type=F32)
            if first:
                rss[w, i - 1, :, cols] = own_term.astype(BF16)
            else:
                term[:, cols] = own_term
        if not first:
            for h in (0, 1):
                scatter_copy(w, h, i - 1).wait_recv()
                side = slice(h * half, (h + 1) * half)
                for cols in spans:
                    total = term[side, cols] + rsr[w, i - 2, side, cols].astype(F32)
                    if out is None:
                        rss[w, i - 1, side, cols] = total.astype(BF16)
                    else:
                        out[0, side, cols] = total.astype(BF16)
                if out is None:
                    scatter_copy(w, h, i).start()
        else:
            for h in (0, 1):
                scatter_copy(w, h, i).start()

    for h in (0, 1):
        gather_copy(GATE, h, last, arriving=True).wait_recv()
    accumulate(GATE, arrx, nz - 1)
    for h in (0, 1):
        gather_copy(UP, h, last, arriving=True).wait_recv()
    accumulate(UP, arrx, nz - 1)

    @pl.loop(0, rows // tile)
    def _(r):
        rows_now = pl.ds(pl.multiple_of(r * tile, tile), tile)
        _, u, _, active = gating(rows_now)
        act[DOWN, rows_now, :] = (active * u).astype(BF16)

    scatter_step(DOWN, 1, first=True)
    for h in (0, 1):
        gather_copy(DOWN, h, last, arriving=True).wait_recv()
    accumulate_down(nz - 1, nz)

    @pl.loop(0, rows // tile)
    def _(r):
        rows_now = pl.ds(pl.multiple_of(r * tile, tile), tile)
        g, u, sig, active = gating(rows_now)
        d = pre[DOWN, rows_now, :]
        slope = sig * (1.0 + g * (1.0 - sig))
        act[GATE, rows_now, :] = (d * u * slope).astype(BF16)
        act[UP, rows_now, :] = (d * active).astype(BF16)

    @pl.loop(0, 2)
    def _(w):
        scatter_step(w, 1, first=True)

    def times_transposed(left, w, n):
        return lax.dot_general(
            left, wfull[w, columns(n), :], (((1,), (1,)), ((), ())), preferred_element_type=F32
        )

    @pl.loop(0, width // WIDE)
    def _(n):
        prod[:, columns(n)] = times_transposed(act[DOWN], DOWN, n).astype(BF16)

    send_rows(prod, ret, 2)

    def input_back():
        @pl.loop(0, width // WIDE)
        def _(n):
            total = times_transposed(act[GATE], GATE, n) + times_transposed(act[UP], UP, n)
            back[:, columns(n)] = total.astype(BF16)

        send_rows(back, retb, 3)

    slots = lax.broadcasted_iota(jnp.int32, (tok_dev, rows), 1)

    def column(row):
        return jnp.broadcast_to(row, (tok_dev, tok_dev)).T[:, 0:1]

    def picks():
        tgt = ids[...] * cap + places[...]
        return [
            jnp.where(slots == column(tgt[k : k + 1, :]), 1.0, 0.0).astype(BF16) for k in (0, 1)
        ]

    def combine_out():
        await_rows(prod, ret, 2)
        pick0, pick1 = picks()
        gate0, gate1 = column(gate_l[0:1, :]), column(gate_l[1:2, :])
        zero = jnp.zeros((tok_dev, 1), F32)

        def step(n, sums):
            cols = columns(n)
            r0 = jnp.dot(pick0, ret[:, cols], preferred_element_type=F32)
            r1 = jnp.dot(pick1, ret[:, cols], preferred_element_type=F32)
            lo[:, cols] = (gate0 * r0 + gate1 * r1).astype(BF16)
            cot = gout[:, cols].astype(F32)
            return (
                sums[0] + jnp.sum(r0 * cot, axis=1, keepdims=True),
                sums[1] + jnp.sum(r1 * cot, axis=1, keepdims=True),
            )

        d0, d1 = lax.fori_loop(0, width // WIDE, step, (zero, zero))
        for k, d in enumerate((d0, d1)):
            gg[k : k + 1, :] = jnp.broadcast_to(d, (tok_dev, tok_dev)).T[0:1, :]

    def combine_back():
        await_rows(back, retb, 3)
        pick0, pick1 = picks()

        @pl.loop(0, width // WIDE)
        def _(n):
            cols = columns(n)
            both = pick0 + pick1
            gt[:, cols] = jnp.dot(both, retb[:, cols], preferred_element_type=F32).astype(BF16)

    back_at = 9
    out_at = 3 * (nz - 3) + 3

    @pl.loop(3, 3 * (nz - 1))
    def _(k):
        @pl.when(k == back_at)
        def _():
            input_back()

        @pl.when(k == out_at)
        def _():
            combine_out()

        scatter_step(lax.rem(k + 2, 3), k // 3 + 1)

    combine_back()

    @pl.loop(1, ne)
    def _(o):
        for k, (src, dst) in enumerate(((outx, arrx), (outg, arrg), (prod, ret), (back, retb))):
            exchange(src, dst, k, o).wait_send()

    def sent(s, gathered):
        for w in (GATE, UP, DOWN):
            for h in (0, 1):
                if gathered:
                    gather_copy(w, h, s).wait_send()
                else:
                    scatter_copy(w, h, s + 1).wait_send()

    @pl.loop(0, nz - 1)
    def _(s):
        sent(s, True)

    @pl.loop(0, nz - 2)
    def _(s):
        sent(s, False)

    for w, out in ((DOWN, od), (GATE, og), (UP, ou)):
        scatter_step(w, nz, out=out)
    sent(nz - 2, False)


def write_kernel(*refs):
    sems = refs[-1]
    count = (len(refs) - 1) // 2
    copies = [
        pltpu.make_async_copy(refs[k], refs[count + k], sems.at[k]) for k in range(count)
    ]
    for copy in copies:
        copy.start()
    for copy in copies:
        copy.wait()


def on_device(tokens, expert_ids, slot_index, routing_gates, grad_out, w_gate, w_up, w_down):
    tok_dev, top_k = expert_ids.shape
    width = tokens.shape[1]
    _, shard, hidden_units = w_gate.shape
    nz, ne = lax.axis_size("dp"), lax.axis_size("expert")
    cap = 2 * tok_dev * top_k // ne
    rows = ne * cap
    nc, nx = (2, 4) if ne % 8 == 0 else (1, ne)
    vmem = pl.BlockSpec(memory_space=pltpu.VMEM)
    held = pl.BlockSpec(memory_space=pl.ANY)
    wide = lambda *lead: pltpu.VMEM((*lead, width), BF16)
    dma = pltpu.SemaphoreType.DMA
    outs = (
        (tokens.shape, BF16),
        (tokens.shape, BF16),
        ((top_k, tok_dev), F32),
        (w_gate.shape, BF16),
        (w_gate.shape, BF16),
        (w_gate.shape, BF16),
    )
    results = pl.pallas_call(
        functools.partial(layer_kernel, nz, ne, nx, nc, cap),
        out_shape=tuple(pltpu.VMEM(*out) for out in outs),
        in_specs=[held] * 8,
        out_specs=[vmem] * 6,
        scratch_shapes=[
            pltpu.VMEM((3, width, hidden_units), BF16),
            wide(rows), wide(rows), wide(rows), wide(rows),
            pltpu.VMEM((3, rows, hidden_units), F32),
            pltpu.VMEM((3, rows, hidden_units), BF16),
            wide(rows), wide(rows), wide(rows), wide(rows),
            pltpu.VMEM((2, width, rows), BF16),
            pltpu.VMEM((3, nz - 1, shard, hidden_units), BF16),
            pltpu.VMEM((3, nz - 1, shard, hidden_units), BF16),
            pltpu.VMEM((rows, tok_dev), BF16),
            pltpu.VMEM((rows, 128), F32),
            pltpu.VMEM((shard, hidden_units), F32),
            wide(tok_dev), wide(tok_dev),
            pltpu.VMEM((top_k, tok_dev), jnp.int32), pltpu.VMEM((top_k, tok_dev), jnp.int32),
            pltpu.VMEM((top_k, tok_dev), F32),
            pltpu.SemaphoreType.REGULAR((8,)),
            dma((3,)), dma((5,)),
            dma((3, 2, nz - 1)), dma((3, 2, nz - 1)), dma((3, 2, nz - 1)), dma((3, 2, nz - 1)),
            dma((4, ne)), dma((4, ne)),
        ],
        compiler_params=pltpu.CompilerParams(
            collective_id=0, has_side_effects=True, vmem_limit_bytes=LIMIT
        ),
    )(expert_ids.T, slot_index.T, routing_gates.T, tokens, grad_out, w_gate, w_up, w_down)
    layer_out, grad_tokens, grad_gates, *grads = pl.pallas_call(
        write_kernel,
        out_shape=tuple(jax.ShapeDtypeStruct(*out) for out in outs),
        in_specs=[vmem] * 6,
        out_specs=[held] * 6,
        scratch_shapes=[dma((6,))],
        compiler_params=pltpu.CompilerParams(vmem_limit_bytes=4 << 20),
    )(*results)
    return layer_out, grad_tokens, grad_gates.T, *grads


def solution(mesh):
    row = P(("dp", "expert"), None)
    weight = P("expert", "dp", None)
    return jax.shard_map(
        on_device,
        mesh=mesh,
        in_specs=(row,) * 5 + (weight,) * 3,
        out_specs=(row,) * 3 + (weight,) * 3,
        check_vma=False,
    )
```
